32 devices in a mesh: inb: 4 (over y, x), outb: 8 (over z, core).
Axes of the slice: x: 2, y: 2, z: 4, core: 2. Of those that a mesh axis runs over, the one named last changes fastest.
Arguments:
- site_cores: float32 [2, 4, 8192, 8192], P(None, None, 'inb', 'outb')
- left_env: float32 [512, 8192], P(None, 'outb')
- outcomes: int32 [2, 512], replicated, may hold values from 0 to 3
Outputs:
- env_out: float32 [512, 8192], P('inb', 'outb')
- probabilities: float32 [2, 4, 512], P(None, None, 'inb')
- log_scale: float32 [512], P('inb')
The draws below stay inside these ranges and needn't reach their ends.
All inputs are finite; a program needn't handle non-finite values.
Results may differ from the reference program's by a relative error of at most 0.00014.
Values sent between devices are 32-bit elements; how exact they have to be, the bound alone decides.
A program may use at most 128 MiB of HBM per device.

```python
import math
import jax
import jax.numpy as jnp
from jax import lax

CHI = 8192
PHYS = 4
SITES = 2
SAMPLES = 512


def draw_site_cores(key, part):
    base_key = jax.random.fold_in(key, 11)
    entry_key = jax.random.fold_in(base_key, 1)
    scale_key = jax.random.fold_in(base_key, 2)
    entries = jax.random.normal(entry_key, (SITES, PHYS, CHI, CHI), jnp.float32)
    spread = math.log(4.0)
    group_scale = jnp.exp(jax.random.uniform(scale_key, (SITES, PHYS, 1, CHI // 64), jnp.float32, 0.0, spread))
    column_scale = jnp.repeat(group_scale, 64, axis=3)
    column_ramp = 1.0 + 2.0 * jnp.arange(CHI, dtype=jnp.float32) / CHI
    return entries * column_scale * column_ramp / math.sqrt(CHI)


def draw_left_env(key, part):
    base_key = jax.random.fold_in(key, 23)
    entries = jax.random.normal(jax.random.fold_in(base_key, 1), (SAMPLES, CHI), jnp.float32)
    return entries


def place_ends(array, key, smallest, largest):
    place = [jax.random.randint(jax.random.fold_in(key, axis), (), 0, length) for axis, length in enumerate(array.shape)]
    widest = array.shape.index(max(array.shape))
    neighbour = place[:widest] + [(place[widest] + 1) % array.shape[widest]] + place[widest + 1:]
    return array.at[tuple(place)].set(smallest).at[tuple(neighbour)].set(largest)


def setup_inputs(seed: int = 0) -> dict:
    key_list = jax.random.split(jax.random.key(seed), 4)
    site_cores = draw_site_cores(jax.random.fold_in(key_list[3], 71), 0)
    left_env = draw_left_env(jax.random.fold_in(key_list[3], 71), 0)
    outcomes = place_ends(jax.random.randint(key_list[2], (SITES, SAMPLES), 0, PHYS), jax.random.fold_in(key_list[2], 1), 0, PHYS - 1).astype(jnp.int32)
    return dict(site_cores=site_cores, left_env=left_env, outcomes=outcomes)


epsilon = 1e-06

def reference(site_cores, left_env, outcomes):
    env = left_env
    log_scale = jnp.zeros((SAMPLES,), jnp.float32)
    prob_list = []
    levels = jnp.arange(PHYS, dtype=jnp.int32)
    for site_index in range(SITES):
        candidates = jnp.einsum('sc,pcd->psd', env, site_cores[site_index], precision=lax.Precision.HIGHEST)
        mean_squares = lax.optimization_barrier(jnp.sum(candidates * candidates, axis=2)) / CHI + epsilon
        prob_list.append(mean_squares / lax.optimization_barrier(jnp.sum(mean_squares, axis=0, keepdims=True)))
        onehot = (outcomes[site_index][None, :] == levels[:, None]).astype(jnp.float32)
        chosen = lax.optimization_barrier(jnp.sum(onehot[:, :, None] * candidates, axis=0))
        chosen_mean = lax.optimization_barrier(jnp.sum(onehot * mean_squares, axis=0))
        env = chosen * lax.rsqrt(chosen_mean)[:, None]
        log_scale = log_scale + 0.5 * jnp.log(chosen_mean)
    return (env, jnp.stack(prob_list), log_scale)
```

```python
import functools

import jax
import jax.numpy as jnp
from jax import lax
from jax.experimental import pallas as pl
from jax.experimental.pallas import tpu as pltpu
from jax.sharding import PartitionSpec as P

epsilon = 1e-06
MESH = pl.DeviceIdType.MESH
LANES = 128
LEAD = 3


def sites_kernel(
    dims, x_ref, cores_ref, code_ref, env_ref, stat_ref,
    env, halves, high, low, stage, part, first, second, squares, scale, norm_out, norm_in, block_stat,
    stat_in, tile, tile_in, own, side, env_sent, first_sent, first_got, second_sent, second_got,
    norm_sent, norm_got, staged, stat_sent, stat_got, tile_sent, tile_got,
):
    owners, outs, group, rows, chunks, tiles, wide, bond = dims
    depth = halves.shape[1]
    groups = wide // LANES
    per_block = chunks // owners
    steps = 2 * chunks + 2
    me_in, me_out = lax.axis_index("inb"), lax.axis_index("outb")
    place, member = lax.div(me_out, group), lax.rem(me_out, group)
    source = place == me_in
    distance = jnp.abs(place - me_in)
    ahead = jnp.logical_and(place >= me_in, place < owners - 1)
    behind = jnp.logical_and(place <= me_in, place > 0)
    low_bit, high_bit = lax.rem(me_in, 2), lax.div(me_in, 2)
    across_x = me_in + 1 - 2 * low_bit
    across_y = lax.rem(me_in + 2, 4)

    def local(ref, sem):
        return pltpu.make_async_copy(ref, ref, sem)

    def remote(source_ref, target_ref, send, recv, in_index, out_index):
        return pltpu.make_async_remote_copy(
            src_ref=source_ref, dst_ref=target_ref, send_sem=send, recv_sem=recv,
            device_id=(in_index, out_index), device_id_type=MESH,
        )

    barrier = pltpu.get_barrier_semaphore()
    for step in range(1, owners):
        pl.semaphore_signal(
            barrier, inc=1, device_id=(lax.rem(me_in + step, owners), me_out), device_id_type=MESH
        )
    for step in range(1, outs):
        pl.semaphore_signal(
            barrier, inc=1, device_id=(me_in, lax.rem(me_out + step, outs)), device_id_type=MESH
        )

    def fetch(site, index):
        slot = lax.rem(index, 2)
        n, p = lax.div(index, 4), lax.rem(index, 4)
        cols = pl.ds(pl.multiple_of(n * wide, wide), wide)
        return pltpu.make_async_copy(cores_ref.at[site, p, :, cols], stage.at[slot], staged.at[slot])

    def convert(site, index, total):
        slot = lax.rem(index, 2)
        n, p = lax.div(index, 4), lax.rem(index, 4)
        fetch(site, index).wait()

        def some(k, carry):
            span = pl.ds(pl.multiple_of(k * LANES, LANES), LANES)
            value = stage[slot, span, :]
            top = value.astype(jnp.bfloat16)
            high[n, p, span, :] = top
            low[n, p, span, :] = (value - top.astype(jnp.float32)).astype(jnp.bfloat16)
            return carry

        lax.fori_loop(0, depth // LANES, some, 0)

        @pl.when(index + 2 < total)
        def _():
            fetch(site, index + 2).start()

    def load_own(m, n):
        return pltpu.make_async_copy(
            x_ref.at[pl.ds(pl.multiple_of(m * rows, rows), rows), pl.ds(pl.multiple_of(n * wide, wide), wide)],
            env.at[0, m, member, n], own.at[0, m, n],
        )

    def pass_on(site, m, n):
        piece = env.at[site, m, member, n]

        @pl.when(ahead)
        def _():
            remote(piece, piece, env_sent.at[site, 0], own.at[site, m, n], me_in, me_out + group).start()

        @pl.when(behind)
        def _():
            remote(piece, piece, env_sent.at[site, 1], own.at[site, m, n], me_in, me_out - group).start()

        for step in range(1, group):
            remote(
                piece, piece, env_sent.at[site, 1 + step], side.at[site, m, member],
                me_in, place * group + lax.rem(member + step, group),
            ).start()

    def forward_first(m, n):
        local(env.at[0, m, member, n], own.at[0, m, n]).wait()
        pass_on(0, m, n)

    total_tiles = tiles * 4
    fetch(0, 0).start()
    fetch(0, 1).start()

    @pl.when(source)
    def _():
        def every(g, carry):
            load_own(lax.div(g, tiles), lax.rem(g, tiles)).start()
            return carry

        lax.fori_loop(0, chunks * tiles, every, 0)

    squares[...] = jnp.zeros_like(squares)
    pl.semaphore_wait(barrier, owners + outs - 2)

    @pl.when(source)
    def _():
        def every(g, carry):
            forward_first(lax.div(g, tiles), lax.rem(g, tiles))
            return carry

        lax.fori_loop(0, LEAD * tiles, every, 0)

    def prepare(index, carry):
        convert(0, index, total_tiles)

        @pl.when(jnp.logical_and(lax.rem(index, 4) == 3, jnp.logical_not(source)))
        def _():
            forward_first(0, lax.div(index, 4))

        return carry

    lax.fori_loop(0, total_tiles, prepare, 0)
    lead = jnp.where(source, LEAD, 1)

    def bits(n):
        kind = lax.rem(n, 2)
        return kind, jnp.where(kind == 0, across_x, across_y), jnp.where(kind == 0, across_y, across_x)

    def send_first(u, n):
        _, partner, _ = bits(n)
        return remote(
            part.at[lax.rem(u, 2), n, pl.ds(0, 2)], first.at[lax.rem(u, 4), n],
            first_sent.at[lax.rem(u, 2), n], first_got.at[lax.rem(u, 4), n], partner, me_out,
        )

    def send_second(u, n):
        _, _, partner = bits(n)
        return remote(
            part.at[lax.rem(u, 2), n, 2], second.at[lax.rem(u, 2), n],
            second_sent.at[lax.rem(u, 2), n], second_got.at[lax.rem(u, 2), n], partner, me_out,
        )

    def send_norm(m, step):
        return remote(
            norm_out.at[m], norm_in.at[m, me_in], norm_sent.at[step], norm_got.at[m, me_in],
            lax.rem(me_in + step, owners), me_out,
        )

    def row_of(columns):
        spare = LANES - columns.shape[0]
        if spare:
            columns = jnp.concatenate([columns, jnp.zeros((spare, LANES), jnp.float32)], axis=0)
        return jnp.sum(columns.T, axis=0, keepdims=True)

    def finish_scale(m):
        for step in range(1, owners):
            origin = lax.rem(me_in + step, owners)
            local(norm_in.at[m, origin], norm_got.at[m, origin]).wait()
        total = norm_out[m, 0:1, :] * 0.0
        for index in range(owners):
            total = total + norm_in[m, index, 0:1, :]
        value = lax.rsqrt(total / bond + epsilon)
        scale[...] = jnp.broadcast_to(value, (LANES, LANES)).T[0:rows]

    def complete(u, n):
        local(second.at[lax.rem(u, 2), n], second_got.at[lax.rem(u, 2), n]).wait()
        send_first(u, n).wait_send()
        send_second(u, n).wait_send()
        value = part[lax.rem(u, 2), n, 3] + second[lax.rem(u, 2), n]
        site, m = lax.div(u, chunks), lax.rem(u, chunks)

        @pl.when(site == 0)
        def _():
            line = value[:, 0:LANES] * value[:, 0:LANES]
            for g in range(1, groups):
                piece = value[:, g * LANES : (g + 1) * LANES]
                line = line + piece * piece
            squares[0, m] = squares[0, m] + line

            @pl.when(source)
            def _():
                env[1, m, member, n] = value

        @pl.when(site == 1)
        def _():
            @pl.when(n == 0)
            def _():
                finish_scale(m)

            line = squares[1, m]
            factor = scale[...]
            for g in range(groups):
                piece = value[:, g * LANES : (g + 1) * LANES] * factor
                line = line + piece * piece
                second[lax.rem(u, 2), n, :, g * LANES : (g + 1) * LANES] = piece
            squares[1, m] = line

            @pl.when(lax.div(m, per_block) == me_in)
            def _():
                span = pl.ds(pl.multiple_of(lax.rem(m, per_block) * rows, rows), rows)
                cols = pl.ds(pl.multiple_of(n * wide, wide), wide)
                env_ref[span, cols] = second[lax.rem(u, 2), n]

    def split(u):
        site, m = lax.div(u, chunks), lax.rem(u, chunks)
        for step in range(1, group):
            other = lax.rem(member + step, group)
            local(env.at[site, m, other], side.at[site, m, other]).wait()
        norm = jnp.zeros((rows, LANES), jnp.float32)
        for g in range(group):
            for n in range(tiles):
                value = env[site, m, g, n]
                top = value.astype(jnp.bfloat16)
                start = (g * tiles + n) * wide
                halves[0:rows, start : start + wide] = top
                halves[rows : 2 * rows, start : start + wide] = (value - top.astype(jnp.float32)).astype(jnp.bfloat16)
                for l in range(groups):
                    piece = value[:, l * LANES : (l + 1) * LANES]
                    norm = norm + piece * piece

        @pl.when(site == 1)
        def _():
            row = jnp.broadcast_to(row_of(norm), (8, LANES))
            norm_out[m] = row
            norm_in[m, me_in] = row
            for step in range(1, owners):
                send_norm(m, step).start()

    def multiply(u, n):
        site, m = lax.div(u, chunks), lax.rem(u, chunks)
        kind, _, _ = bits(n)
        terms = []
        for p in range(4):
            both = jnp.dot(halves[...], high[n, p], preferred_element_type=jnp.float32)
            rest = jnp.dot(halves[0:rows], low[n, p], preferred_element_type=jnp.float32)
            terms.append(both[0:rows] + (both[rows : 2 * rows] + rest))
        code = code_ref[site, m]
        odd, far = lax.rem(code, 2) == 1, code >= 2
        slot = lax.rem(u, 2)
        for g in range(groups):
            now = [t[:, g * LANES : (g + 1) * LANES] for t in terms]
            now = [jnp.where(odd, now[(q + 1) % 4], now[q]) for q in range(4)]
            now = [jnp.where(far, now[(q + 2) % 4], now[q]) for q in range(4)]
            for q in range(4):
                rel_low, rel_high = lax.rem(low_bit + q % 2, 2), lax.rem(high_bit + q // 2, 2)
                a = jnp.where(kind == 0, rel_low, rel_high)
                b = jnp.where(kind == 0, rel_high, rel_low)
                part[slot, n, 2 * (1 - a) + (1 - b), :, g * LANES : (g + 1) * LANES] = now[q]
        send_first(u, n).start()

    def merge(u, n):
        local(first.at[lax.rem(u, 4), n], first_got.at[lax.rem(u, 4), n]).wait()
        slot = lax.rem(u, 2)
        part[slot, n, 2] = part[slot, n, 2] + first[lax.rem(u, 4), n, 0]
        send_second(u, n).start()
        part[slot, n, 3] = part[slot, n, 3] + first[lax.rem(u, 4), n, 1]

    def one(f, carry):
        u, n = lax.div(f, tiles), lax.rem(f, tiles)

        @pl.when(u >= 2)
        def _():
            complete(u - 2, n)

        far = u - 2 - distance

        @pl.when(jnp.logical_and(far >= 0, far < chunks))
        def _():
            @pl.when(jnp.logical_not(source))
            def _():
                local(env.at[1, far, member, n], own.at[1, far, n]).wait()

            pass_on(1, far, n)

        @pl.when(u < 2 * chunks)
        def _():
            @pl.when(n == 0)
            def _():
                split(u)

            @pl.when(jnp.logical_and(u == chunks - 1, n == 0))
            def _():
                fetch(1, 0).start()
                fetch(1, 1).start()

            multiply(u, n)

        @pl.when(u + lead < chunks)
        def _():
            forward_first(u + lead, n)

        @pl.when(jnp.logical_and(u >= 1, u <= 2 * chunks))
        def _():
            merge(u - 1, n)

        @pl.when(u == chunks - 1)
        def _():
            def again(p, carry):
                convert(1, n * 4 + p, total_tiles)
                return carry

            lax.fori_loop(0, 4, again, 0)

        return carry

    lax.fori_loop(0, steps * tiles, one, 0)

    block_stat[...] = jnp.zeros_like(block_stat)
    for site in range(2):
        for block in range(owners):
            line = jnp.concatenate([squares[site, block * per_block + j] for j in range(per_block)], axis=0)
            block_stat[block, site : site + 1, :] = row_of(line)

    def send_stat(step):
        target = lax.rem(me_in + step, owners)
        return remote(
            block_stat.at[target], stat_in.at[me_in], stat_sent.at[step], stat_got.at[me_in], target, me_out
        )

    for step in range(1, owners):
        send_stat(step).start()
    stat_in[me_in] = block_stat[me_in]
    for step in range(1, owners):
        origin = lax.rem(me_in + step, owners)
        local(stat_in.at[origin], stat_got.at[origin]).wait()
    for r in range(owners):
        tile[r : r + 1, :] = stat_in[lax.rem(place + r, owners), 0:1, :]
        tile[owners + r : owners + r + 1, :] = stat_in[lax.rem(me_in + r, owners), 1:2, :]

    def send_tile(step):
        return remote(
            tile, tile_in.at[me_out], tile_sent.at[step], tile_got.at[me_out],
            me_in, lax.rem(me_out + step, outs),
        )

    for step in range(1, outs):
        send_tile(step).start()
    tile_in[me_out] = tile[...]
    for step in range(1, outs):
        origin = lax.rem(me_out + step, outs)
        local(tile_in.at[origin], tile_got.at[origin]).wait()
    total = tile_in[0]
    for index in range(1, outs):
        total = total + tile_in[index]
    stat_ref[...] = total

    for step in range(1, owners):
        send_stat(step).wait_send()
        local(norm_out, norm_sent.at[step]).wait()
    for step in range(1, outs):
        send_tile(step).wait_send()
    for site in range(2):
        whole = env.at[site, :, member]

        @pl.when(ahead)
        def _():
            local(whole, env_sent.at[site, 0]).wait()

        @pl.when(behind)
        def _():
            local(whole, env_sent.at[site, 1]).wait()

        for step in range(1, group):
            local(whole, env_sent.at[site, 1 + step]).wait()


def on_device(owners, outs, site_cores, left_env, outcomes):
    samples, width = left_env.shape
    sites, count, depth = site_cores.shape[:3]
    group = outs // owners
    block = samples // owners
    rows = block // 2
    chunks = samples // rows
    wide = max(LANES, width // 4)
    tiles = width // wide
    bond = width * outs
    assert sites == 2 and count == owners == 4 and block == LANES and depth == group * width
    me_in, place = lax.axis_index("inb"), lax.axis_index("outb") // group
    offsets = jnp.stack([jnp.full((samples,), place, jnp.int32), jnp.arange(samples, dtype=jnp.int32) // block])
    code = lax.rem(outcomes + owners - offsets, owners)
    code = jnp.broadcast_to(code.reshape(sites, chunks, rows, 1), (sites, chunks, rows, LANES))
    f32, bf16 = jnp.float32, jnp.bfloat16
    dma = pltpu.SemaphoreType.DMA
    dims = (owners, outs, group, rows, chunks, tiles, wide, bond)
    env_raw, stats = pl.pallas_call(
        functools.partial(sites_kernel, dims),
        out_shape=(jax.ShapeDtypeStruct((block, width), f32), jax.ShapeDtypeStruct((2 * owners, LANES), f32)),
        in_specs=[
            pl.BlockSpec(memory_space=pl.ANY), pl.BlockSpec(memory_space=pl.ANY),
            pl.BlockSpec(memory_space=pltpu.VMEM),
        ],
        out_specs=(pl.BlockSpec(memory_space=pltpu.VMEM), pl.BlockSpec(memory_space=pltpu.VMEM)),
        scratch_shapes=[
            pltpu.VMEM((2, chunks, group, tiles, rows, wide), f32),
            pltpu.VMEM((2 * rows, depth), bf16),
            pltpu.VMEM((tiles, count, depth, wide), bf16),
            pltpu.VMEM((tiles, count, depth, wide), bf16),
            pltpu.VMEM((2, depth, wide), f32),
            pltpu.VMEM((2, tiles, 4, rows, wide), f32),
            pltpu.VMEM((4, tiles, 2, rows, wide), f32),
            pltpu.VMEM((2, tiles, rows, wide), f32),
            pltpu.VMEM((2, chunks, rows, LANES), f32),
            pltpu.VMEM((rows, LANES), f32),
            pltpu.VMEM((chunks, 8, LANES), f32),
            pltpu.VMEM((chunks, owners, 8, LANES), f32),
            pltpu.VMEM((owners, 8, LANES), f32),
            pltpu.VMEM((owners, 8, LANES), f32),
            pltpu.VMEM((2 * owners, LANES), f32),
            pltpu.VMEM((outs, 2 * owners, LANES), f32),
            dma((2, chunks, tiles)), dma((2, chunks, group)), dma((2, 1 + group)),
            dma((2, tiles)), dma((4, tiles)), dma((2, tiles)), dma((2, tiles)),
            dma((owners,)), dma((chunks, owners)), dma((2,)),
            dma((owners,)), dma((owners,)), dma((outs,)), dma((outs,)),
        ],
        compiler_params=pltpu.CompilerParams(
            collective_id=0, has_side_effects=True, vmem_limit_bytes=60 * 1024 * 1024
        ),
        cost_estimate=pl.CostEstimate(
            flops=12 * samples * depth * count * width, bytes_accessed=8 * count * depth * width, transcendentals=0
        ),
        name="sites",
    )(left_env, site_cores, code)

    mean_squares = stats.reshape(sites, owners, LANES) / bond + epsilon
    shares = mean_squares / jnp.sum(mean_squares, axis=1, keepdims=True)
    ids = lax.dynamic_slice_in_dim(outcomes, me_in * block, block, 1)
    levels = jnp.arange(count, dtype=jnp.int32)
    turn = lax.rem(levels[None, :, None] + count - ids[:, None, :], count)
    probs = jnp.zeros_like(shares)
    for r in range(owners):
        probs = jnp.where(turn == r, shares[:, r : r + 1], probs)
    chosen = mean_squares[:, 0]
    log_scale = 0.5 * jnp.log(chosen[0]) + 0.5 * jnp.log(chosen[1])
    env_out = env_raw * lax.rsqrt(chosen[1])[:, None]
    return (env_out, probs, log_scale)


def solution(mesh):
    in_specs = (P(None, None, "inb", "outb"), P(None, "outb"), P())
    out_specs = (P("inb", "outb"), P(None, None, "inb"), P("inb"))
    return jax.shard_map(
        functools.partial(on_device, mesh.shape["inb"], mesh.shape["outb"]),
        mesh=mesh, in_specs=in_specs, out_specs=out_specs, check_vma=False,
    )
```

```python
import functools

import jax
import jax.numpy as jnp
from jax import lax
from jax.experimental import pallas as pl
from jax.experimental.pallas import tpu as pltpu
from jax.sharding import PartitionSpec as P

epsilon = 1e-06
MESH = pl.DeviceIdType.MESH
LANES = 128
AHEAD = 4
HOP = 2
MERGE = 2
RING = 8
PIECES = 16


def sites_kernel(
    dims, x_ref, cores_ref, code_ref, env_ref, stat_ref,
    env, halves, high, low, stage, part, first, second, squares, scale, norm_out, norm_in, block_stat,
    stat_in, tile, tile_in, own, side, open_own, open_side, env_sent, first_sent, first_got, second_sent, second_got,
    norm_sent, norm_got, staged, stat_sent, stat_got, tile_sent, tile_got,
):
    owners, outs, group, rows, chunks, tiles, wide, bond, lag = dims
    depth = halves.shape[1]
    groups = wide // LANES
    per_block = chunks // owners
    part_rows = rows // 2
    slots = 2 * chunks * tiles
    me_in, me_out = lax.axis_index("inb"), lax.axis_index("outb")
    place, member = lax.div(me_out, group), lax.rem(me_out, group)
    source = place == me_in
    distance = jnp.abs(place - me_in)
    ahead = jnp.logical_and(place >= me_in, place < owners - 1)
    behind = jnp.logical_and(place <= me_in, place > 0)
    low_bit, high_bit = lax.rem(me_in, 2), lax.div(me_in, 2)
    across_x = me_in + 1 - 2 * low_bit
    across_y = lax.rem(me_in + 2, 4)

    def local(ref, sem):
        return pltpu.make_async_copy(ref, ref, sem)

    def remote(source_ref, target_ref, send, recv, in_index, out_index):
        return pltpu.make_async_remote_copy(
            src_ref=source_ref, dst_ref=target_ref, send_sem=send, recv_sem=recv,
            device_id=(in_index, out_index), device_id_type=MESH,
        )

    barrier = pltpu.get_barrier_semaphore()
    for step in range(1, owners):
        pl.semaphore_signal(
            barrier, inc=1, device_id=(lax.rem(me_in + step, owners), me_out), device_id_type=MESH
        )
    for step in range(1, outs):
        pl.semaphore_signal(
            barrier, inc=1, device_id=(me_in, lax.rem(me_out + step, outs)), device_id_type=MESH
        )

    jobs = tiles * 4

    def fetch(job):
        index, slot = lax.rem(job, jobs), lax.rem(job, 2)
        n, p = lax.div(index, 4), lax.rem(index, 4)
        cols = pl.ds(pl.multiple_of(n * wide, wide), wide)
        return pltpu.make_async_copy(
            cores_ref.at[lax.div(job, jobs), p, :, cols], stage.at[slot], staged.at[slot]
        )

    def convert(job):
        slot, p = lax.rem(job, 2), lax.rem(job, 4)
        hold = lax.rem(lax.div(job, 4), tiles + 1)
        fetch(job).wait()

        def some(k, carry):
            span = pl.ds(pl.multiple_of(k * LANES, LANES), LANES)
            value = stage[slot, span, :]
            top = value.astype(jnp.bfloat16)
            high[hold, p, span, :] = top
            low[hold, p, span, :] = (value - top.astype(jnp.float32)).astype(jnp.bfloat16)
            return carry

        lax.fori_loop(0, depth // LANES, some, 0)

        @pl.when(job + 2 < 2 * jobs)
        def _():
            fetch(job + 2).start()

    def load_own(m, n):
        return pltpu.make_async_copy(
            x_ref.at[pl.ds(pl.multiple_of(m * rows, rows), rows), pl.ds(pl.multiple_of(n * wide, wide), wide)],
            env.at[0, m, member, n], own.at[0, m, n],
        )

    def load_open(h, n):
        span = pl.ds(pl.multiple_of(h * part_rows, part_rows), part_rows)
        return pltpu.make_async_copy(
            x_ref.at[span, pl.ds(pl.multiple_of(n * wide, wide), wide)],
            env.at[0, 0, member, n, span], open_own.at[h, n],
        )

    def pass_on(site, piece, got, side_got):
        @pl.when(ahead)
        def _():
            remote(piece, piece, env_sent.at[site, 0], got, me_in, me_out + group).start()

        @pl.when(behind)
        def _():
            remote(piece, piece, env_sent.at[site, 1], got, me_in, me_out - group).start()

        for step in range(1, group):
            remote(
                piece, piece, env_sent.at[site, 1 + step], side_got,
                me_in, place * group + lax.rem(member + step, group),
            ).start()

    def forward_chunk(site, m, n):
        pass_on(site, env.at[site, m, member, n], own.at[site, m, n], side.at[site, m, member])

    def forward_first(m, n):
        local(env.at[0, m, member, n], own.at[0, m, n]).wait()
        forward_chunk(0, m, n)

    def forward_open(q):
        h, n = lax.div(q, tiles), lax.rem(q, tiles)
        piece = env.at[0, 0, member, n, pl.ds(pl.multiple_of(h * part_rows, part_rows), part_rows)]
        local(piece, open_own.at[h, n]).wait()
        pass_on(0, piece, open_own.at[h, n], open_side.at[h, member])

    fetch(0).start()
    fetch(1).start()

    @pl.when(source)
    def _():
        def opening(q, carry):
            load_open(lax.div(q, tiles), lax.rem(q, tiles)).start()
            return carry

        lax.fori_loop(0, 2 * tiles, opening, 0)

        def every(g, carry):
            load_own(lax.div(g, tiles), lax.rem(g, tiles)).start()
            return carry

        lax.fori_loop(tiles, chunks * tiles, every, 0)

    pl.semaphore_wait(barrier, owners + outs - 2)

    squares[...] = jnp.zeros_like(squares)

    def prepare(job, carry):
        convert(job)

        @pl.when(lax.rem(job, 2) == 1)
        def _():
            forward_open(lax.div(job, 2))

        return carry

    lax.fori_loop(0, jobs, prepare, 0)
    extra = jnp.where(source, AHEAD, jnp.maximum(owners - 1 - distance, 0))

    def bits(n):
        kind = lax.rem(n, 2)
        return kind, jnp.where(kind == 0, across_x, across_y), jnp.where(kind == 0, across_y, across_x)

    def send_first(f, start=0, count=None):
        _, partner, _ = bits(lax.rem(f, tiles))
        span = pl.ds(start, rows if count is None else count)
        return remote(
            part.at[lax.rem(f, lag), pl.ds(0, 2), span], first.at[lax.rem(f, RING), :, span],
            first_sent.at[lax.rem(f, lag)], first_got.at[lax.rem(f, RING)], partner, me_out,
        )

    def send_second(f):
        _, _, partner = bits(lax.rem(f, tiles))
        return remote(
            part.at[lax.rem(f, lag), 2], second.at[lax.rem(f, RING)],
            second_sent.at[lax.rem(f, lag)], second_got.at[lax.rem(f, RING)], partner, me_out,
        )

    def send_norm(m, step):
        return remote(
            norm_out.at[m], norm_in.at[m, me_in], norm_sent.at[step], norm_got.at[m, me_in],
            lax.rem(me_in + step, owners), me_out,
        )

    def row_of(columns):
        spare = LANES - columns.shape[0]
        if spare:
            columns = jnp.concatenate([columns, jnp.zeros((spare, LANES), jnp.float32)], axis=0)
        return jnp.sum(columns.T, axis=0, keepdims=True)

    def finish_scale(m):
        for step in range(1, owners):
            origin = lax.rem(me_in + step, owners)
            local(norm_in.at[m, origin], norm_got.at[m, origin]).wait()
        total = norm_out[m, 0:1, :] * 0.0
        for index in range(owners):
            total = total + norm_in[m, index, 0:1, :]
        value = lax.rsqrt(total / bond + epsilon)
        scale[...] = jnp.broadcast_to(value, (LANES, LANES)).T[0:rows]

    def place_of(f):
        u = lax.div(f, tiles)
        return lax.div(u, chunks), lax.rem(u, chunks), lax.rem(f, tiles)

    def complete(f):
        slot, ring = lax.rem(f, lag), lax.rem(f, RING)
        local(second.at[ring], second_got.at[ring]).wait()
        send_first(f).wait_send()
        send_second(f).wait_send()
        site, m, n = place_of(f)

        @pl.when(site == 0)
        def _():
            line = squares[0, m]
            for g in range(groups):
                cols = slice(g * LANES, (g + 1) * LANES)
                piece = part[slot, 3, :, cols] + second[ring, :, cols]
                line = line + piece * piece
                part[slot, 3, :, cols] = piece
            squares[0, m] = line

            @pl.when(source)
            def _():
                env[1, m, member, n] = part[slot, 3]

        @pl.when(site == 1)
        def _():
            @pl.when(n == 0)
            def _():
                finish_scale(m)

            line = squares[1, m]
            factor = scale[...]
            for g in range(groups):
                cols = slice(g * LANES, (g + 1) * LANES)
                piece = (part[slot, 3, :, cols] + second[ring, :, cols]) * factor
                line = line + piece * piece
                part[slot, 3, :, cols] = piece
            squares[1, m] = line

            @pl.when(lax.div(m, per_block) == me_in)
            def _():
                span = pl.ds(pl.multiple_of(lax.rem(m, per_block) * rows, rows), rows)
                cols = pl.ds(pl.multiple_of(n * wide, wide), wide)
                env_ref[span, cols] = part[slot, 3]

    def split(site, m, start, count):
        norm = jnp.zeros((count, LANES), jnp.float32)
        for g in range(group):
            for n in range(tiles):
                value = env[site, m, g, n, start : start + count, :]
                top = value.astype(jnp.bfloat16)
                column = (g * tiles + n) * wide
                halves[0:count, column : column + wide] = top
                halves[count : 2 * count, column : column + wide] = (value - top.astype(jnp.float32)).astype(jnp.bfloat16)
                for l in range(groups):
                    piece = value[:, l * LANES : (l + 1) * LANES]
                    norm = norm + piece * piece
        return norm

    def split_chunk(site, m):
        for step in range(1, group):
            other = lax.rem(member + step, group)
            local(env.at[site, m, other], side.at[site, m, other]).wait()
        norm = split(site, m, 0, rows)

        @pl.when(site == 1)
        def _():
            row = jnp.broadcast_to(row_of(norm), (8, LANES))
            norm_out[m] = row
            norm_in[m, me_in] = row
            for step in range(1, owners):
                send_norm(m, step).start()

    def multiply(f, start, count):
        site, m, n = place_of(f)
        kind, _, _ = bits(n)
        hold = lax.rem(site * tiles + n, tiles + 1)
        terms = []
        for p in range(4):
            both = jnp.dot(halves[0 : 2 * count], high[hold, p], preferred_element_type=jnp.float32)
            rest = jnp.dot(halves[0:count], low[hold, p], preferred_element_type=jnp.float32)
            terms.append(both[0:count] + (both[count : 2 * count] + rest))
        code = code_ref[site, m, start : start + count, :]
        odd, far = lax.rem(code, 2) == 1, code >= 2
        slot = lax.rem(f, lag)
        for g in range(groups):
            now = [t[:, g * LANES : (g + 1) * LANES] for t in terms]
            now = [jnp.where(odd, now[(q + 1) % 4], now[q]) for q in range(4)]
            now = [jnp.where(far, now[(q + 2) % 4], now[q]) for q in range(4)]
            for q in range(4):
                rel_low, rel_high = lax.rem(low_bit + q % 2, 2), lax.rem(high_bit + q // 2, 2)
                a = jnp.where(kind == 0, rel_low, rel_high)
                b = jnp.where(kind == 0, rel_high, rel_low)
                part[slot, 2 * (1 - a) + (1 - b), start : start + count, g * LANES : (g + 1) * LANES] = now[q]
        send_first(f, start, count).start()

    def merge(f):
        slot, ring = lax.rem(f, lag), lax.rem(f, RING)
        local(first.at[ring], first_got.at[ring]).wait()
        part[slot, 2] = part[slot, 2] + first[ring, 0]
        send_second(f).start()
        part[slot, 3] = part[slot, 3] + first[ring, 1]

    for h in range(2):
        span = pl.ds(h * part_rows, part_rows)
        for step in range(1, group):
            other = lax.rem(member + step, group)
            local(env.at[0, 0, other, :, span], open_side.at[h, other]).wait()
        split(0, 0, h * part_rows, part_rows)

        def opening(f, carry):
            multiply(f, h * part_rows, part_rows)
            tick = h * tiles + f

            def early(k, carry):
                due = jnp.minimum(2 * k + jnp.where(source, 0, 2 * distance + 1), 2 * tiles - 1)

                @pl.when(jnp.logical_and(k < extra, due == tick))
                def _():
                    forward_first(lax.div(tiles + k, tiles), lax.rem(tiles + k, tiles))

                return carry

            lax.fori_loop(0, AHEAD, early, 0)
            return carry

        lax.fori_loop(0, tiles, opening, 0)

    turn = (chunks - 1) * tiles

    def one(f, carry):
        site, m, n = place_of(f)

        @pl.when(f >= lag)
        def _():
            complete(f - lag)

        @pl.when(jnp.logical_and(f >= tiles, f < slots))
        def _():
            @pl.when(n == 0)
            def _():
                split_chunk(site, m)

            multiply(f, 0, rows)

        back = jnp.where(f < tiles, 0, MERGE)

        @pl.when(jnp.logical_or(f < tiles, jnp.logical_and(f >= tiles + MERGE, f < slots + MERGE)))
        def _():
            merge(f - back)

        far = f - lag - HOP * distance

        @pl.when(jnp.logical_and(far >= 0, far < chunks * tiles))
        def _():
            far_m, far_n = lax.div(far, tiles), lax.rem(far, tiles)

            @pl.when(jnp.logical_not(source))
            def _():
                local(env.at[1, far_m, member, far_n], own.at[1, far_m, far_n]).wait()

            forward_chunk(1, far_m, far_n)

        ready = f + tiles + extra

        @pl.when(ready < chunks * tiles)
        def _():
            forward_first(lax.div(ready, tiles), lax.rem(ready, tiles))

        @pl.when(jnp.logical_and(f >= turn - 4, f < turn))
        def _():
            convert(jobs + f - (turn - 4))

        @pl.when(jnp.logical_and(f >= turn, f < turn + 2 * (tiles - 1)))
        def _():
            def again(k, carry):
                convert(jobs + 4 + 2 * (f - turn) + k)
                return carry

            lax.fori_loop(0, 2, again, 0)

        return carry

    lax.fori_loop(0, slots + lag, one, 0)

    block_stat[...] = jnp.zeros_like(block_stat)
    for site in range(2):
        for block in range(owners):
            line = jnp.concatenate([squares[site, block * per_block + j] for j in range(per_block)], axis=0)
            block_stat[block, site : site + 1, :] = row_of(line)

    def send_stat(step):
        target = lax.rem(me_in + step, owners)
        return remote(
            block_stat.at[target], stat_in.at[me_in], stat_sent.at[step], stat_got.at[me_in], target, me_out
        )

    for step in range(1, owners):
        send_stat(step).start()
    stat_in[me_in] = block_stat[me_in]
    for step in range(1, owners):
        origin = lax.rem(me_in + step, owners)
        local(stat_in.at[origin], stat_got.at[origin]).wait()
    for r in range(owners):
        tile[r : r + 1, :] = stat_in[lax.rem(place + r, owners), 0:1, :]
        tile[owners + r : owners + r + 1, :] = stat_in[lax.rem(me_in + r, owners), 1:2, :]

    def send_tile(step):
        return remote(
            tile, tile_in.at[me_out], tile_sent.at[step], tile_got.at[me_out],
            me_in, lax.rem(me_out + step, outs),
        )

    for step in range(1, outs):
        send_tile(step).start()
    tile_in[me_out] = tile[...]
    for step in range(1, outs):
        origin = lax.rem(me_out + step, outs)
        local(tile_in.at[origin], tile_got.at[origin]).wait()
    total = tile_in[0]
    for index in range(1, outs):
        total = total + tile_in[index]
    stat_ref[...] = total

    for step in range(1, owners):
        send_stat(step).wait_send()
        local(norm_out, norm_sent.at[step]).wait()
    for step in range(1, outs):
        send_tile(step).wait_send()
    for site in range(2):
        whole = env.at[site, :, member]

        @pl.when(ahead)
        def _():
            local(whole, env_sent.at[site, 0]).wait()

        @pl.when(behind)
        def _():
            local(whole, env_sent.at[site, 1]).wait()

        for step in range(1, group):
            local(whole, env_sent.at[site, 1 + step]).wait()


def on_device(owners, outs, site_cores, left_env, outcomes):
    samples, width = left_env.shape
    sites, count, depth = site_cores.shape[:3]
    group = outs // owners
    block = samples // owners
    wide = max(LANES, width // 4)
    tiles = width // wide
    chunks = max(owners, PIECES // tiles)
    rows = samples // chunks
    bond = width * outs
    lag = 5
    assert chunks * tiles >= tiles + lag + HOP * (owners - 1) and sites == 2 and count == owners == 4 and block == LANES and depth == group * width
    me_in, place = lax.axis_index("inb"), lax.axis_index("outb") // group
    offsets = jnp.stack([jnp.full((samples,), place, jnp.int32), jnp.arange(samples, dtype=jnp.int32) // block])
    code = lax.rem(outcomes + owners - offsets, owners)
    code = jnp.broadcast_to(code.reshape(sites, chunks, rows, 1), (sites, chunks, rows, LANES))
    f32, bf16 = jnp.float32, jnp.bfloat16
    dma = pltpu.SemaphoreType.DMA
    dims = (owners, outs, group, rows, chunks, tiles, wide, bond, lag)
    env_raw, stats = pl.pallas_call(
        functools.partial(sites_kernel, dims),
        out_shape=(jax.ShapeDtypeStruct((block, width), f32), jax.ShapeDtypeStruct((2 * owners, LANES), f32)),
        in_specs=[
            pl.BlockSpec(memory_space=pl.ANY), pl.BlockSpec(memory_space=pl.ANY),
            pl.BlockSpec(memory_space=pltpu.VMEM),
        ],
        out_specs=(pl.BlockSpec(memory_space=pltpu.VMEM), pl.BlockSpec(memory_space=pltpu.VMEM)),
        scratch_shapes=[
            pltpu.VMEM((2, chunks, group, tiles, rows, wide), f32),
            pltpu.VMEM((2 * rows, depth), bf16),
            pltpu.VMEM((tiles + 1, count, depth, wide), bf16),
            pltpu.VMEM((tiles + 1, count, depth, wide), bf16),
            pltpu.VMEM((2, depth, wide), f32),
            pltpu.VMEM((lag, 4, rows, wide), f32),
            pltpu.VMEM((RING, 2, rows, wide), f32),
            pltpu.VMEM((RING, rows, wide), f32),
            pltpu.VMEM((2, chunks, rows, LANES), f32),
            pltpu.VMEM((rows, LANES), f32),
            pltpu.VMEM((chunks, 8, LANES), f32),
            pltpu.VMEM((chunks, owners, 8, LANES), f32),
            pltpu.VMEM((owners, 8, LANES), f32),
            pltpu.VMEM((owners, 8, LANES), f32),
            pltpu.VMEM((2 * owners, LANES), f32),
            pltpu.VMEM((outs, 2 * owners, LANES), f32),
            dma((2, chunks, tiles)), dma((2, chunks, group)), dma((2, tiles)), dma((2, group)), dma((2, 1 + group)),
            dma((lag,)), dma((RING,)), dma((lag,)), dma((RING,)),
            dma((owners,)), dma((chunks, owners)), dma((2,)),
            dma((owners,)), dma((owners,)), dma((outs,)), dma((outs,)),
        ],
        compiler_params=pltpu.CompilerParams(
            collective_id=0, has_side_effects=True, vmem_limit_bytes=62 * 1024 * 1024
        ),
        cost_estimate=pl.CostEstimate(
            flops=12 * samples * depth * count * width, bytes_accessed=8 * count * depth * width, transcendentals=0
        ),
        name="sites",
    )(left_env, site_cores, code)

    mean_squares = stats.reshape(sites, owners, LANES) / bond + epsilon
    shares = mean_squares / jnp.sum(mean_squares, axis=1, keepdims=True)
    ids = lax.dynamic_slice_in_dim(outcomes, me_in * block, block, 1)
    levels = jnp.arange(count, dtype=jnp.int32)
    turn = lax.rem(levels[None, :, None] + count - ids[:, None, :], count)
    probs = jnp.zeros_like(shares)
    for r in range(owners):
        probs = jnp.where(turn == r, shares[:, r : r + 1], probs)
    chosen = mean_squares[:, 0]
    log_scale = 0.5 * jnp.log(chosen[0]) + 0.5 * jnp.log(chosen[1])
    env_out = env_raw * lax.rsqrt(chosen[1])[:, None]
    return (env_out, probs, log_scale)


def solution(mesh):
    in_specs = (P(None, None, "inb", "outb"), P(None, "outb"), P())
    out_specs = (P("inb", "outb"), P(None, None, "inb"), P("inb"))
    return jax.shard_map(
        functools.partial(on_device, mesh.shape["inb"], mesh.shape["outb"]),
        mesh=mesh, in_specs=in_specs, out_specs=out_specs, check_vma=False,
    )
```

```python
import functools

import jax
import jax.numpy as jnp
from jax import lax
from jax.experimental import pallas as pl
from jax.experimental.pallas import tpu as pltpu
from jax.sharding import PartitionSpec as P

epsilon = 1e-06
MESH = pl.DeviceIdType.MESH
LANES = 128
HOP = 2
MERGE = 2
RING = 8
PIECES = 16


def sites_kernel(
    dims, x_ref, cores_ref, outcome_ref, env_ref, stat_ref,
    env, code, halves, high, low, stage, part, first, second, squares, scale, norm_out, norm_in, block_stat,
    stat_in, tile, tile_in, own, side, open_own, open_side, env_sent, first_sent, first_got, second_sent, second_got,
    norm_sent, norm_got, staged, stat_sent, stat_got, tile_sent, tile_got,
):
    owners, outs, group, rows, chunks, tiles, wide, bond, lag = dims
    depth = halves.shape[1]
    groups = wide // LANES
    per_block = chunks // owners
    part_rows = rows // 2
    slots = 2 * chunks * tiles
    me_in, me_out = lax.axis_index("inb"), lax.axis_index("outb")
    place, member = lax.div(me_out, group), lax.rem(me_out, group)
    source = place == me_in
    distance = jnp.abs(place - me_in)
    ahead = jnp.logical_and(place >= me_in, place < owners - 1)
    behind = jnp.logical_and(place <= me_in, place > 0)
    low_bit, high_bit = lax.rem(me_in, 2), lax.div(me_in, 2)
    across_x = me_in + 1 - 2 * low_bit
    across_y = lax.rem(me_in + 2, 4)

    def local(ref, sem):
        return pltpu.make_async_copy(ref, ref, sem)

    def remote(source_ref, target_ref, send, recv, in_index, out_index):
        return pltpu.make_async_remote_copy(
            src_ref=source_ref, dst_ref=target_ref, send_sem=send, recv_sem=recv,
            device_id=(in_index, out_index), device_id_type=MESH,
        )

    barrier = pltpu.get_barrier_semaphore()
    for step in range(1, owners):
        pl.semaphore_signal(
            barrier, inc=1, device_id=(lax.rem(me_in + step, owners), me_out), device_id_type=MESH
        )
    for step in range(1, outs):
        pl.semaphore_signal(
            barrier, inc=1, device_id=(me_in, lax.rem(me_out + step, outs)), device_id_type=MESH
        )

    jobs = tiles * 4

    def fetch(job):
        index, slot = lax.rem(job, jobs), lax.rem(job, 2)
        n, p = lax.div(index, 4), lax.rem(index, 4)
        cols = pl.ds(pl.multiple_of(n * wide, wide), wide)
        return pltpu.make_async_copy(
            cores_ref.at[lax.div(job, jobs), p, :, cols], stage.at[slot], staged.at[slot]
        )

    def convert(job):
        slot, p = lax.rem(job, 2), lax.rem(job, 4)
        hold = lax.rem(lax.div(job, 4), tiles + 1)
        fetch(job).wait()

        def some(k, carry):
            span = pl.ds(pl.multiple_of(k * LANES, LANES), LANES)
            value = stage[slot, span, :]
            top = value.astype(jnp.bfloat16)
            high[hold, p, span, :] = top
            low[hold, p, span, :] = (value - top.astype(jnp.float32)).astype(jnp.bfloat16)
            return carry

        lax.fori_loop(0, depth // LANES, some, 0)

        @pl.when(job + 2 < 2 * jobs)
        def _():
            fetch(job + 2).start()

    def load_own(m, n):
        return pltpu.make_async_copy(
            x_ref.at[pl.ds(pl.multiple_of(m * rows, rows), rows), pl.ds(pl.multiple_of(n * wide, wide), wide)],
            env.at[0, m, member, n], own.at[0, m, n],
        )

    def half_of(h):
        return pl.ds(pl.multiple_of(lax.rem(h, 2) * part_rows, part_rows), part_rows)

    def load_open(q):
        h, n = lax.div(q, tiles), lax.rem(q, tiles)
        span = pl.ds(pl.multiple_of(h * part_rows, part_rows), part_rows)
        return pltpu.make_async_copy(
            x_ref.at[span, pl.ds(pl.multiple_of(n * wide, wide), wide)],
            env.at[0, lax.div(h, 2), member, n, half_of(h)], open_own.at[h, n],
        )

    def pass_on(site, piece, got, side_got):
        @pl.when(ahead)
        def _():
            remote(piece, piece, env_sent.at[site, 0], got, me_in, me_out + group).start()

        @pl.when(behind)
        def _():
            remote(piece, piece, env_sent.at[site, 1], got, me_in, me_out - group).start()

        for step in range(1, group):
            remote(
                piece, piece, env_sent.at[site, 1 + step], side_got,
                me_in, place * group + lax.rem(member + step, group),
            ).start()

    def forward_chunk(site, m, n):
        pass_on(site, env.at[site, m, member, n], own.at[site, m, n], side.at[site, m, member])

    def forward_first(m, n):
        local(env.at[0, m, member, n], own.at[0, m, n]).wait()
        forward_chunk(0, m, n)

    def forward_piece(k):
        m = 2 + lax.div(k, tiles)

        @pl.when(m < chunks)
        def _():
            forward_first(m, lax.rem(k, tiles))

    def forward_open(q):
        h, n = lax.div(q, tiles), lax.rem(q, tiles)
        piece = env.at[0, lax.div(h, 2), member, n, half_of(h)]
        local(piece, open_own.at[h, n]).wait()
        pass_on(0, piece, open_own.at[h, n], open_side.at[h, member])

    fetch(0).start()
    fetch(1).start()

    @pl.when(source)
    def _():
        def opening(q, carry):
            load_open(q).start()
            return carry

        lax.fori_loop(0, 4 * tiles, opening, 0)

        def every(g, carry):
            load_own(lax.div(g, tiles), lax.rem(g, tiles)).start()
            return carry

        lax.fori_loop(2 * tiles, chunks * tiles, every, 0)

    pl.semaphore_wait(barrier, owners + outs - 2)

    squares[...] = jnp.zeros_like(squares)

    def prepare(job, carry):
        convert(job)

        @pl.when(source)
        def _():
            forward_open(job)

        turn_now = job - 1 - 3 * distance

        @pl.when(jnp.logical_not(source))
        def _():
            @pl.when(jnp.logical_and(turn_now >= 0, lax.rem(turn_now + 2, 2) == 0))
            def _():
                forward_open(lax.div(turn_now, 2))

        return carry

    lax.fori_loop(0, jobs, prepare, 0)
    done = jnp.where(source, jobs, lax.div(jnp.maximum(jobs - 3 * distance, 0), 2))
    base = jnp.maximum(done, tiles)

    def forward_next(count):
        @pl.when(base + count < jobs)
        def _():
            forward_open(base + count)

        @pl.when(base + count >= jobs)
        def _():
            forward_piece(base + count - jobs)

    def bits(n):
        kind = lax.rem(n, 2)
        return kind, jnp.where(kind == 0, across_x, across_y), jnp.where(kind == 0, across_y, across_x)

    def send_first(f, start=0, count=None):
        _, partner, _ = bits(lax.rem(f, tiles))
        span = pl.ds(start, rows if count is None else count)
        return remote(
            part.at[lax.rem(f, lag), pl.ds(0, 2), span], first.at[lax.rem(f, RING), :, span],
            first_sent.at[lax.rem(f, lag)], first_got.at[lax.rem(f, RING)], partner, me_out,
        )

    def send_second(f):
        _, _, partner = bits(lax.rem(f, tiles))
        return remote(
            part.at[lax.rem(f, lag), 2], second.at[lax.rem(f, RING)],
            second_sent.at[lax.rem(f, lag)], second_got.at[lax.rem(f, RING)], partner, me_out,
        )

    def send_norm(m, step):
        return remote(
            norm_out.at[m], norm_in.at[m, me_in], norm_sent.at[step], norm_got.at[m, me_in],
            lax.rem(me_in + step, owners), me_out,
        )

    def row_of(columns):
        spare = LANES - columns.shape[0]
        if spare:
            columns = jnp.concatenate([columns, jnp.zeros((spare, LANES), jnp.float32)], axis=0)
        return jnp.sum(columns.T, axis=0, keepdims=True)

    def finish_scale(m):
        for step in range(1, owners):
            origin = lax.rem(me_in + step, owners)
            local(norm_in.at[m, origin], norm_got.at[m, origin]).wait()
        total = norm_out[m, 0:1, :] * 0.0
        for index in range(owners):
            total = total + norm_in[m, index, 0:1, :]
        value = lax.rsqrt(total / bond + epsilon)
        scale[...] = jnp.broadcast_to(value, (LANES, LANES)).T[0:rows]

    def place_of(f):
        u = lax.div(f, tiles)
        return lax.div(u, chunks), lax.rem(u, chunks), lax.rem(f, tiles)

    def complete(f):
        slot, ring = lax.rem(f, lag), lax.rem(f, RING)
        local(second.at[ring], second_got.at[ring]).wait()
        send_first(f).wait_send()
        send_second(f).wait_send()
        site, m, n = place_of(f)

        @pl.when(site == 0)
        def _():
            line = squares[0, m]
            for g in range(groups):
                cols = slice(g * LANES, (g + 1) * LANES)
                piece = part[slot, 3, :, cols] + second[ring, :, cols]
                line = line + piece * piece
                part[slot, 3, :, cols] = piece
            squares[0, m] = line

            @pl.when(source)
            def _():
                env[1, m, member, n] = part[slot, 3]

        @pl.when(site == 1)
        def _():
            @pl.when(n == 0)
            def _():
                finish_scale(m)

            line = squares[1, m]
            factor = scale[...]
            for g in range(groups):
                cols = slice(g * LANES, (g + 1) * LANES)
                piece = (part[slot, 3, :, cols] + second[ring, :, cols]) * factor
                line = line + piece * piece
                part[slot, 3, :, cols] = piece
            squares[1, m] = line

            @pl.when(lax.div(m, per_block) == me_in)
            def _():
                span = pl.ds(pl.multiple_of(lax.rem(m, per_block) * rows, rows), rows)
                cols = pl.ds(pl.multiple_of(n * wide, wide), wide)
                env_ref[span, cols] = part[slot, 3]

    def split(site, m, start, count):
        row = outcome_ref[site, m].astype(jnp.float32)
        offset = jnp.where(site == 0, place, lax.div(m, per_block))
        turned = jnp.broadcast_to(row, (LANES, rows)).T.astype(jnp.int32) + (owners - offset)
        code[...] = lax.rem(turned, owners)
        norm = jnp.zeros((count, LANES), jnp.float32)
        for g in range(group):
            for n in range(tiles):
                value = env[site, m, g, n, start : start + count, :]
                top = value.astype(jnp.bfloat16)
                column = (g * tiles + n) * wide
                halves[0:count, column : column + wide] = top
                halves[count : 2 * count, column : column + wide] = (value - top.astype(jnp.float32)).astype(jnp.bfloat16)
                for l in range(groups):
                    piece = value[:, l * LANES : (l + 1) * LANES]
                    norm = norm + piece * piece
        return norm

    def split_chunk(site, m):
        halved = jnp.logical_and(site == 0, m == 1)
        for step in range(1, group):
            other = lax.rem(member + step, group)

            @pl.when(jnp.logical_not(halved))
            def _():
                local(env.at[site, m, other], side.at[site, m, other]).wait()

            @pl.when(halved)
            def _():
                for h in range(2):
                    span = pl.ds(h * part_rows, part_rows)
                    local(env.at[0, 1, other, :, span], open_side.at[2 + h, other]).wait()
        norm = split(site, m, 0, rows)

        @pl.when(site == 1)
        def _():
            row = jnp.broadcast_to(row_of(norm), (8, LANES))
            norm_out[m] = row
            norm_in[m, me_in] = row
            for step in range(1, owners):
                send_norm(m, step).start()

    def multiply(f, start, count):
        site, m, n = place_of(f)
        kind, _, _ = bits(n)
        hold = lax.rem(site * tiles + n, tiles + 1)
        terms = []
        for p in range(4):
            both = jnp.dot(halves[0 : 2 * count], high[hold, p], preferred_element_type=jnp.float32)
            rest = jnp.dot(halves[0:count], low[hold, p], preferred_element_type=jnp.float32)
            terms.append(both[0:count] + (both[count : 2 * count] + rest))
        shift = code[start : start + count, :]
        odd, far = lax.rem(shift, 2) == 1, shift >= 2
        slot = lax.rem(f, lag)
        for g in range(groups):
            now = [t[:, g * LANES : (g + 1) * LANES] for t in terms]
            now = [jnp.where(odd, now[(q + 1) % 4], now[q]) for q in range(4)]
            now = [jnp.where(far, now[(q + 2) % 4], now[q]) for q in range(4)]
            for q in range(4):
                rel_low, rel_high = lax.rem(low_bit + q % 2, 2), lax.rem(high_bit + q // 2, 2)
                a = jnp.where(kind == 0, rel_low, rel_high)
                b = jnp.where(kind == 0, rel_high, rel_low)
                part[slot, 2 * (1 - a) + (1 - b), start : start + count, g * LANES : (g + 1) * LANES] = now[q]
        send_first(f, start, count).start()

    def merge(f):
        slot, ring = lax.rem(f, lag), lax.rem(f, RING)
        local(first.at[ring], first_got.at[ring]).wait()
        part[slot, 2] = part[slot, 2] + first[ring, 0]
        send_second(f).start()
        part[slot, 3] = part[slot, 3] + first[ring, 1]

    def rest_open(q, carry):
        forward_open(q)
        return carry

    lax.fori_loop(done, tiles, rest_open, 0)
    for h in range(2):
        span = pl.ds(h * part_rows, part_rows)
        for step in range(1, group):
            other = lax.rem(member + step, group)
            local(env.at[0, 0, other, :, span], open_side.at[h, other]).wait()
        split(0, 0, h * part_rows, part_rows)

        def opening(f, carry):
            multiply(f, h * part_rows, part_rows)

            forward_next(h * tiles + f)
            return carry

        lax.fori_loop(0, tiles, opening, 0)

    turn = (chunks - 1) * tiles

    def one(f, carry):
        site, m, n = place_of(f)

        @pl.when(f >= lag)
        def _():
            complete(f - lag)

        @pl.when(jnp.logical_and(f >= tiles, f < slots))
        def _():
            @pl.when(n == 0)
            def _():
                split_chunk(site, m)

            multiply(f, 0, rows)

        back = jnp.where(f < tiles, 0, MERGE)

        @pl.when(jnp.logical_or(f < tiles, jnp.logical_and(f >= tiles + MERGE, f < slots + MERGE)))
        def _():
            merge(f - back)

        far = f - lag - HOP * distance

        @pl.when(jnp.logical_and(far >= 0, far < chunks * tiles))
        def _():
            far_m, far_n = lax.div(far, tiles), lax.rem(far, tiles)

            @pl.when(jnp.logical_not(source))
            def _():
                local(env.at[1, far_m, member, far_n], own.at[1, far_m, far_n]).wait()

            forward_chunk(1, far_m, far_n)

        forward_next(2 * tiles + f)

        @pl.when(jnp.logical_and(f >= turn - 4, f < turn))
        def _():
            convert(jobs + f - (turn - 4))

        @pl.when(jnp.logical_and(f >= turn, f < turn + 2 * (tiles - 1)))
        def _():
            def again(k, carry):
                convert(jobs + 4 + 2 * (f - turn) + k)
                return carry

            lax.fori_loop(0, 2, again, 0)

        return carry

    lax.fori_loop(0, slots + lag, one, 0)

    block_stat[...] = jnp.zeros_like(block_stat)
    for site in range(2):
        for block in range(owners):
            line = jnp.concatenate([squares[site, block * per_block + j] for j in range(per_block)], axis=0)
            block_stat[block, site : site + 1, :] = row_of(line)

    def send_stat(step):
        target = lax.rem(me_in + step, owners)
        return remote(
            block_stat.at[target], stat_in.at[me_in], stat_sent.at[step], stat_got.at[me_in], target, me_out
        )

    for step in range(1, owners):
        send_stat(step).start()
    stat_in[me_in] = block_stat[me_in]
    for step in range(1, owners):
        origin = lax.rem(me_in + step, owners)
        local(stat_in.at[origin], stat_got.at[origin]).wait()
    for r in range(owners):
        tile[r : r + 1, :] = stat_in[lax.rem(place + r, owners), 0:1, :]
        tile[owners + r : owners + r + 1, :] = stat_in[lax.rem(me_in + r, owners), 1:2, :]

    def send_tile(step):
        return remote(
            tile, tile_in.at[me_out], tile_sent.at[step], tile_got.at[me_out],
            me_in, lax.rem(me_out + step, outs),
        )

    for step in range(1, outs):
        send_tile(step).start()
    tile_in[me_out] = tile[...]
    for step in range(1, outs):
        origin = lax.rem(me_out + step, outs)
        local(tile_in.at[origin], tile_got.at[origin]).wait()
    total = tile_in[0]
    for index in range(1, outs):
        total = total + tile_in[index]
    stat_ref[...] = total

    for step in range(1, owners):
        send_stat(step).wait_send()
        local(norm_out, norm_sent.at[step]).wait()
    for step in range(1, outs):
        send_tile(step).wait_send()
    for site in range(2):
        whole = env.at[site, :, member]

        @pl.when(ahead)
        def _():
            local(whole, env_sent.at[site, 0]).wait()

        @pl.when(behind)
        def _():
            local(whole, env_sent.at[site, 1]).wait()

        for step in range(1, group):
            local(whole, env_sent.at[site, 1 + step]).wait()


def finish_kernel(owners, block, bond, raw_ref, stat_ref, outcome_ref, env_ref, prob_ref, log_ref):
    span = pl.ds(pl.multiple_of(lax.axis_index("inb") * block, block), block)
    means = stat_ref[...] / bond + epsilon
    for site in range(2):
        first = site * owners
        total = means[first : first + 1]
        for r in range(1, owners):
            total = total + means[first + r : first + r + 1]
        ids = outcome_ref[site : site + 1, span]
        for p in range(owners):
            turn = lax.rem(p + owners - ids, owners)
            share = means[first : first + 1]
            for r in range(1, owners):
                share = jnp.where(turn == r, means[first + r : first + r + 1], share)
            prob_ref[site, p : p + 1, :] = share / total
    log_ref[...] = 0.5 * jnp.log(means[0:1]) + 0.5 * jnp.log(means[owners : owners + 1])
    factor = jnp.broadcast_to(lax.rsqrt(means[owners : owners + 1]), (LANES, LANES)).T
    for g in range(raw_ref.shape[1] // LANES):
        cols = slice(g * LANES, (g + 1) * LANES)
        env_ref[:, cols] = raw_ref[:, cols] * factor


def on_device(owners, outs, site_cores, left_env, outcomes):
    samples, width = left_env.shape
    sites, count, depth = site_cores.shape[:3]
    group = outs // owners
    block = samples // owners
    wide = max(LANES, width // 4)
    tiles = width // wide
    chunks = max(owners, PIECES // tiles)
    rows = samples // chunks
    bond = width * outs
    lag = 5
    assert chunks * tiles >= tiles + lag + HOP * (owners - 1) and sites == 2 and count == owners == 4 and block == LANES and depth == group * width
    f32, bf16 = jnp.float32, jnp.bfloat16
    dma = pltpu.SemaphoreType.DMA
    dims = (owners, outs, group, rows, chunks, tiles, wide, bond, lag)
    env_raw, stats = pl.pallas_call(
        functools.partial(sites_kernel, dims),
        out_shape=(jax.ShapeDtypeStruct((block, width), f32), jax.ShapeDtypeStruct((2 * owners, LANES), f32)),
        in_specs=[
            pl.BlockSpec(memory_space=pl.ANY), pl.BlockSpec(memory_space=pl.ANY),
            pl.BlockSpec(memory_space=pltpu.VMEM),
        ],
        out_specs=(pl.BlockSpec(memory_space=pltpu.VMEM), pl.BlockSpec(memory_space=pltpu.VMEM)),
        scratch_shapes=[
            pltpu.VMEM((2, chunks, group, tiles, rows, wide), f32),
            pltpu.VMEM((rows, LANES), jnp.int32),
            pltpu.VMEM((2 * rows, depth), bf16),
            pltpu.VMEM((tiles + 1, count, depth, wide), bf16),
            pltpu.VMEM((tiles + 1, count, depth, wide), bf16),
            pltpu.VMEM((2, depth, wide), f32),
            pltpu.VMEM((lag, 4, rows, wide), f32),
            pltpu.VMEM((RING, 2, rows, wide), f32),
            pltpu.VMEM((RING, rows, wide), f32),
            pltpu.VMEM((2, chunks, rows, LANES), f32),
            pltpu.VMEM((rows, LANES), f32),
            pltpu.VMEM((chunks, 8, LANES), f32),
            pltpu.VMEM((chunks, owners, 8, LANES), f32),
            pltpu.VMEM((owners, 8, LANES), f32),
            pltpu.VMEM((owners, 8, LANES), f32),
            pltpu.VMEM((2 * owners, LANES), f32),
            pltpu.VMEM((outs, 2 * owners, LANES), f32),
            dma((2, chunks, tiles)), dma((2, chunks, group)), dma((4, tiles)), dma((4, group)), dma((2, 1 + group)),
            dma((lag,)), dma((RING,)), dma((lag,)), dma((RING,)),
            dma((owners,)), dma((chunks, owners)), dma((2,)),
            dma((owners,)), dma((owners,)), dma((outs,)), dma((outs,)),
        ],
        compiler_params=pltpu.CompilerParams(
            collective_id=0, has_side_effects=True, vmem_limit_bytes=62 * 1024 * 1024
        ),
        cost_estimate=pl.CostEstimate(
            flops=12 * samples * depth * count * width, bytes_accessed=8 * count * depth * width, transcendentals=0
        ),
        name="sites",
    )(left_env, site_cores, outcomes.reshape(sites, chunks, 1, rows))

    spec = pl.BlockSpec(memory_space=pltpu.VMEM)
    env_out, probs, logs = pl.pallas_call(
        functools.partial(finish_kernel, owners, block, bond),
        out_shape=(
            jax.ShapeDtypeStruct((block, width), f32), jax.ShapeDtypeStruct((sites, count, block), f32),
            jax.ShapeDtypeStruct((1, block), f32),
        ),
        in_specs=[spec] * 3,
        out_specs=(spec,) * 3,
        name="finish",
    )(env_raw, stats, outcomes)
    return (env_out, probs, logs.reshape(block))


def solution(mesh):
    in_specs = (P(None, None, "inb", "outb"), P(None, "outb"), P())
    out_specs = (P("inb", "outb"), P(None, None, "inb"), P("inb"))
    return jax.shard_map(
        functools.partial(on_device, mesh.shape["inb"], mesh.shape["outb"]),
        mesh=mesh, in_specs=in_specs, out_specs=out_specs, check_vma=False,
    )
```

```python
import functools

import jax
import jax.numpy as jnp
from jax import lax
from jax.experimental import pallas as pl
from jax.experimental.pallas import tpu as pltpu
from jax.sharding import PartitionSpec as P

epsilon = 1e-06
MESH = pl.DeviceIdType.MESH
LANES = 128
HOP = 2
MERGE = 2
RING = 8
PIECES = 16


def sites_kernel(
    dims, x_ref, cores_ref, outcome_ref, env_ref, stat_ref,
    env, code, halves, high, low, stage, part, first, second, squares, scale, norm_out, norm_in, block_stat,
    stat_in, tile, tile_in, own, side, open_own, open_side, env_sent, first_sent, first_got, second_sent, second_got,
    norm_sent, norm_got, staged, stat_sent, stat_got, tile_sent, tile_got,
):
    owners, outs, group, rows, chunks, tiles, wide, bond, lag = dims
    depth = halves.shape[1]
    groups = wide // LANES
    per_block = chunks // owners
    part_rows = rows // 2
    slots = 2 * chunks * tiles
    me_in, me_out = lax.axis_index("inb"), lax.axis_index("outb")
    place, member = lax.div(me_out, group), lax.rem(me_out, group)
    source = place == me_in
    distance = jnp.abs(place - me_in)
    ahead = jnp.logical_and(place >= me_in, place < owners - 1)
    behind = jnp.logical_and(place <= me_in, place > 0)
    low_bit, high_bit = lax.rem(me_in, 2), lax.div(me_in, 2)
    across_x = me_in + 1 - 2 * low_bit
    across_y = lax.rem(me_in + 2, 4)

    def local(ref, sem):
        return pltpu.make_async_copy(ref, ref, sem)

    def remote(source_ref, target_ref, send, recv, in_index, out_index):
        return pltpu.make_async_remote_copy(
            src_ref=source_ref, dst_ref=target_ref, send_sem=send, recv_sem=recv,
            device_id=(in_index, out_index), device_id_type=MESH,
        )

    barrier = pltpu.get_barrier_semaphore()
    for step in range(1, owners):
        pl.semaphore_signal(
            barrier, inc=1, device_id=(lax.rem(me_in + step, owners), me_out), device_id_type=MESH
        )
    for step in range(1, outs):
        pl.semaphore_signal(
            barrier, inc=1, device_id=(me_in, lax.rem(me_out + step, outs)), device_id_type=MESH
        )

    jobs = tiles * 4

    def fetch(job):
        index, slot = lax.rem(job, jobs), lax.rem(job, 2)
        n, p = lax.div(index, 4), lax.rem(index, 4)
        cols = pl.ds(pl.multiple_of(n * wide, wide), wide)
        return pltpu.make_async_copy(
            cores_ref.at[lax.div(job, jobs), p, :, cols], stage.at[slot], staged.at[slot]
        )

    def convert(job):
        slot, p = lax.rem(job, 2), lax.rem(job, 4)
        hold = lax.rem(lax.div(job, 4), tiles + 1)
        fetch(job).wait()

        def some(k, carry):
            span = pl.ds(pl.multiple_of(k * LANES, LANES), LANES)
            value = stage[slot, span, :]
            top = value.astype(jnp.bfloat16)
            high[hold, p, span, :] = top
            low[hold, p, span, :] = (value - top.astype(jnp.float32)).astype(jnp.bfloat16)
            return carry

        lax.fori_loop(0, depth // LANES, some, 0)

        @pl.when(job + 2 < 2 * jobs)
        def _():
            fetch(job + 2).start()

    def load_own(m, n):
        return pltpu.make_async_copy(
            x_ref.at[pl.ds(pl.multiple_of(m * rows, rows), rows), pl.ds(pl.multiple_of(n * wide, wide), wide)],
            env.at[0, m, member, n], own.at[0, m, n],
        )

    def half_of(h):
        return pl.ds(pl.multiple_of(lax.rem(h, 2) * part_rows, part_rows), part_rows)

    def load_open(q):
        h, n = lax.div(q, tiles), lax.rem(q, tiles)
        span = pl.ds(pl.multiple_of(h * part_rows, part_rows), part_rows)
        return pltpu.make_async_copy(
            x_ref.at[span, pl.ds(pl.multiple_of(n * wide, wide), wide)],
            env.at[0, lax.div(h, 2), member, n, half_of(h)], open_own.at[h, n],
        )

    def pass_on(site, piece, got, side_got):
        @pl.when(ahead)
        def _():
            remote(piece, piece, env_sent.at[site, 0], got, me_in, me_out + group).start()

        @pl.when(behind)
        def _():
            remote(piece, piece, env_sent.at[site, 1], got, me_in, me_out - group).start()

        for step in range(1, group):
            remote(
                piece, piece, env_sent.at[site, 1 + step], side_got,
                me_in, place * group + lax.rem(member + step, group),
            ).start()

    def forward_chunk(site, m, n):
        pass_on(site, env.at[site, m, member, n], own.at[site, m, n], side.at[site, m, member])

    def forward_first(m, n):
        local(env.at[0, m, member, n], own.at[0, m, n]).wait()
        forward_chunk(0, m, n)

    def forward_piece(k):
        m = 2 + lax.div(k, tiles)

        @pl.when(m < chunks)
        def _():
            forward_first(m, lax.rem(k, tiles))

    def forward_open(q):
        h, n = lax.div(q, tiles), lax.rem(q, tiles)
        piece = env.at[0, lax.div(h, 2), member, n, half_of(h)]
        local(piece, open_own.at[h, n]).wait()
        pass_on(0, piece, open_own.at[h, n], open_side.at[h, member])

    fetch(0).start()
    fetch(1).start()

    @pl.when(source)
    def _():
        def opening(q, carry):
            load_open(q).start()
            return carry

        lax.fori_loop(0, 4 * tiles, opening, 0)

        def every(g, carry):
            load_own(lax.div(g, tiles), lax.rem(g, tiles)).start()
            return carry

        lax.fori_loop(2 * tiles, chunks * tiles, every, 0)

    pl.semaphore_wait(barrier, owners + outs - 2)

    squares[...] = jnp.zeros_like(squares)
    block_stat[...] = jnp.zeros_like(block_stat)

    @pl.when(source)
    def _():
        def opening(q, carry):
            forward_open(q)
            return carry

        lax.fori_loop(0, jobs, opening, 0)

    def prepare(job, carry):
        turn_now = job - 4 * distance

        @pl.when(jnp.logical_and(jnp.logical_not(source), turn_now >= 0))
        def _():
            @pl.when(lax.rem(turn_now, 2) == 0)
            def _():
                forward_open(lax.div(turn_now, 2))

        convert(job)
        return carry

    lax.fori_loop(0, jobs, prepare, 0)
    done = jnp.where(source, jobs, lax.div(jnp.maximum(jobs - 4 * distance + 1, 0), 2))
    base = jnp.maximum(done, tiles)
    last = distance == owners - 1

    def forward_next(count):
        @pl.when(base + count < jobs)
        def _():
            forward_open(base + count)

        @pl.when(base + count >= jobs)
        def _():
            forward_piece(base + count - jobs)

    def bits(n):
        kind = lax.rem(n, 2)
        return kind, jnp.where(kind == 0, across_x, across_y), jnp.where(kind == 0, across_y, across_x)

    def send_first(f, start=0, count=None):
        _, partner, _ = bits(lax.rem(f, tiles))
        span = pl.ds(start, rows if count is None else count)
        return remote(
            part.at[lax.rem(f, lag), pl.ds(0, 2), span], first.at[lax.rem(f, RING), :, span],
            first_sent.at[lax.rem(f, lag)], first_got.at[lax.rem(f, RING)], partner, me_out,
        )

    def send_second(f):
        _, _, partner = bits(lax.rem(f, tiles))
        return remote(
            part.at[lax.rem(f, lag), 2], second.at[lax.rem(f, RING)],
            second_sent.at[lax.rem(f, lag)], second_got.at[lax.rem(f, RING)], partner, me_out,
        )

    def send_norm(m, step):
        return remote(
            norm_out.at[m], norm_in.at[m, me_in], norm_sent.at[step], norm_got.at[m, me_in],
            lax.rem(me_in + step, owners), me_out,
        )

    def row_of(columns):
        spare = LANES - columns.shape[0]
        if spare:
            columns = jnp.concatenate([columns, jnp.zeros((spare, LANES), jnp.float32)], axis=0)
        return jnp.sum(columns.T, axis=0, keepdims=True)

    def finish_scale(m):
        for step in range(1, owners):
            origin = lax.rem(me_in + step, owners)
            local(norm_in.at[m, origin], norm_got.at[m, origin]).wait()
        total = norm_out[m, 0:1, :] * 0.0
        for index in range(owners):
            total = total + norm_in[m, index, 0:1, :]
        value = lax.rsqrt(total / bond + epsilon)
        scale[...] = jnp.broadcast_to(value, (LANES, LANES)).T[0:rows]

    def place_of(f):
        u = lax.div(f, tiles)
        return lax.div(u, chunks), lax.rem(u, chunks), lax.rem(f, tiles)

    def complete(f):
        slot, ring = lax.rem(f, lag), lax.rem(f, RING)
        local(second.at[ring], second_got.at[ring]).wait()
        send_first(f).wait_send()
        send_second(f).wait_send()
        site, m, n = place_of(f)

        @pl.when(site == 0)
        def _():
            line = squares[0, m]
            for g in range(groups):
                cols = slice(g * LANES, (g + 1) * LANES)
                piece = part[slot, 3, :, cols] + second[ring, :, cols]
                line = line + piece * piece
                part[slot, 3, :, cols] = piece
            squares[0, m] = line

            @pl.when(source)
            def _():
                env[1, m, member, n] = part[slot, 3]

        @pl.when(site == 1)
        def _():
            @pl.when(n == 0)
            def _():
                finish_scale(m)

            line = squares[1, m]
            factor = scale[...]
            for g in range(groups):
                cols = slice(g * LANES, (g + 1) * LANES)
                piece = (part[slot, 3, :, cols] + second[ring, :, cols]) * factor
                line = line + piece * piece
                part[slot, 3, :, cols] = piece
            squares[1, m] = line

            @pl.when(lax.div(m, per_block) == me_in)
            def _():
                span = pl.ds(pl.multiple_of(lax.rem(m, per_block) * rows, rows), rows)
                cols = pl.ds(pl.multiple_of(n * wide, wide), wide)
                env_ref[span, cols] = part[slot, 3]

        @pl.when(jnp.logical_and(n == tiles - 1, lax.rem(m, per_block) == per_block - 1))
        def _():
            note_block(site, m)

    def note_block(site, m):
        block = lax.div(m, per_block)
        line = jnp.concatenate([squares[site, block * per_block + j] for j in range(per_block)], axis=0)
        block_stat[block, pl.ds(site, 1), :] = row_of(line)

    def split(site, m, start, count):
        block = lax.div(m, per_block)
        both = outcome_ref[:, pl.ds(pl.multiple_of(block * LANES, LANES), LANES)].astype(jnp.float32)
        row = jnp.where(site == 0, both[0:1], both[1:2])
        offset = jnp.where(site == 0, place, block)
        turned = jnp.broadcast_to(row, (LANES, LANES)).T.astype(jnp.int32) + (owners - offset)
        code[...] = lax.rem(turned, owners)
        norm = jnp.zeros((count, LANES), jnp.float32)
        for g in range(group):
            for n in range(tiles):
                value = env[site, m, g, n, start : start + count, :]
                top = value.astype(jnp.bfloat16)
                column = (g * tiles + n) * wide
                halves[0:count, column : column + wide] = top
                halves[count : 2 * count, column : column + wide] = (value - top.astype(jnp.float32)).astype(jnp.bfloat16)
                for l in range(groups):
                    piece = value[:, l * LANES : (l + 1) * LANES]
                    norm = norm + piece * piece
        return norm

    def split_chunk(site, m):
        halved = jnp.logical_and(site == 0, m == 1)
        for step in range(1, group):
            other = lax.rem(member + step, group)

            @pl.when(jnp.logical_not(halved))
            def _():
                local(env.at[site, m, other], side.at[site, m, other]).wait()

            @pl.when(halved)
            def _():
                for h in range(2):
                    span = pl.ds(h * part_rows, part_rows)
                    local(env.at[0, 1, other, :, span], open_side.at[2 + h, other]).wait()
        norm = split(site, m, 0, rows)

        @pl.when(site == 1)
        def _():
            row = jnp.broadcast_to(row_of(norm), (8, LANES))
            norm_out[m] = row
            norm_in[m, me_in] = row
            for step in range(1, owners):
                send_norm(m, step).start()

    def multiply(f, start, count):
        site, m, n = place_of(f)
        kind, _, _ = bits(n)
        hold = lax.rem(site * tiles + n, tiles + 1)
        terms = []
        for p in range(4):
            both = jnp.dot(halves[0 : 2 * count], high[hold, p], preferred_element_type=jnp.float32)
            rest = jnp.dot(halves[0:count], low[hold, p], preferred_element_type=jnp.float32)
            terms.append(both[0:count] + (both[count : 2 * count] + rest))
        shift = code[pl.ds(pl.multiple_of(lax.rem(m, per_block) * rows, rows) + start, count), :]
        odd, far = lax.rem(shift, 2) == 1, shift >= 2
        slot = lax.rem(f, lag)
        for g in range(groups):
            now = [t[:, g * LANES : (g + 1) * LANES] for t in terms]
            now = [jnp.where(odd, now[(q + 1) % 4], now[q]) for q in range(4)]
            now = [jnp.where(far, now[(q + 2) % 4], now[q]) for q in range(4)]
            for q in range(4):
                rel_low, rel_high = lax.rem(low_bit + q % 2, 2), lax.rem(high_bit + q // 2, 2)
                a = jnp.where(kind == 0, rel_low, rel_high)
                b = jnp.where(kind == 0, rel_high, rel_low)
                part[slot, 2 * (1 - a) + (1 - b), start : start + count, g * LANES : (g + 1) * LANES] = now[q]
        send_first(f, start, count).start()

    def merge(f):
        slot, ring = lax.rem(f, lag), lax.rem(f, RING)
        local(first.at[ring], first_got.at[ring]).wait()
        part[slot, 2] = part[slot, 2] + first[ring, 0]
        send_second(f).start()
        part[slot, 3] = part[slot, 3] + first[ring, 1]

    def rest_open(q, carry):
        forward_open(q)
        return carry

    lax.fori_loop(done, tiles, rest_open, 0)
    for h in range(2):
        span = pl.ds(h * part_rows, part_rows)
        for step in range(1, group):
            other = lax.rem(member + step, group)
            local(env.at[0, 0, other, :, span], open_side.at[h, other]).wait()
        split(0, 0, h * part_rows, part_rows)

        def opening(f, carry):
            multiply(f, h * part_rows, part_rows)

            forward_next(h * tiles + f)
            return carry

        lax.fori_loop(0, tiles, opening, 0)

    turn = (chunks - 1) * tiles

    def one(f, carry):
        site, m, n = place_of(f)

        @pl.when(f >= lag)
        def _():
            complete(f - lag)

        @pl.when(jnp.logical_and(f >= tiles, f < slots))
        def _():
            @pl.when(n == 0)
            def _():
                @pl.when(jnp.logical_and(last, jnp.logical_and(f >= 2 * tiles, site == 0)))
                def _():
                    forward_piece(f - 2 * tiles + tiles - 1)

                split_chunk(site, m)

            multiply(f, 0, rows)

        back = jnp.where(f < tiles, 0, MERGE)

        @pl.when(jnp.logical_or(f < tiles, jnp.logical_and(f >= tiles + MERGE, f < slots + MERGE)))
        def _():
            merge(f - back)

        far = f - lag - HOP * distance

        @pl.when(jnp.logical_and(far >= 0, far < chunks * tiles))
        def _():
            far_m, far_n = lax.div(far, tiles), lax.rem(far, tiles)

            @pl.when(jnp.logical_not(source))
            def _():
                local(env.at[1, far_m, member, far_n], own.at[1, far_m, far_n]).wait()

            forward_chunk(1, far_m, far_n)

        @pl.when(jnp.logical_or(jnp.logical_not(last), f < tiles))
        def _():
            forward_next(2 * tiles + f)

        @pl.when(jnp.logical_and(last, jnp.logical_and(n == tiles - 1, f >= 2 * tiles - 1)))
        def _():
            def several(k, carry):
                forward_piece(f + 1 - 2 * tiles + k)
                return carry

            lax.fori_loop(0, tiles - 1, several, 0)

        @pl.when(jnp.logical_and(f >= turn - 4, f < turn))
        def _():
            convert(jobs + f - (turn - 4))

        @pl.when(jnp.logical_and(f >= turn, f < turn + 2 * (tiles - 1)))
        def _():
            def again(k, carry):
                convert(jobs + 4 + 2 * (f - turn) + k)
                return carry

            lax.fori_loop(0, 2, again, 0)

        return carry

    lax.fori_loop(0, slots + lag, one, 0)

    def send_stat(step):
        target = lax.rem(me_in + step, owners)
        return remote(
            block_stat.at[target], stat_in.at[me_in], stat_sent.at[step], stat_got.at[me_in], target, me_out
        )

    for step in range(1, owners):
        send_stat(step).start()
    stat_in[me_in] = block_stat[me_in]
    for step in range(1, owners):
        origin = lax.rem(me_in + step, owners)
        local(stat_in.at[origin], stat_got.at[origin]).wait()
    for r in range(owners):
        tile[r : r + 1, :] = stat_in[lax.rem(place + r, owners), 0:1, :]
        tile[owners + r : owners + r + 1, :] = stat_in[lax.rem(me_in + r, owners), 1:2, :]

    def send_tile(step):
        return remote(
            tile, tile_in.at[me_out], tile_sent.at[step], tile_got.at[me_out],
            me_in, lax.rem(me_out + step, outs),
        )

    for step in range(1, outs):
        send_tile(step).start()
    tile_in[me_out] = tile[...]
    for step in range(1, outs):
        origin = lax.rem(me_out + step, outs)
        local(tile_in.at[origin], tile_got.at[origin]).wait()
    total = tile_in[0]
    for index in range(1, outs):
        total = total + tile_in[index]
    stat_ref[...] = total

    for step in range(1, owners):
        send_stat(step).wait_send()
        local(norm_out, norm_sent.at[step]).wait()
    for step in range(1, outs):
        send_tile(step).wait_send()
    for site in range(2):
        whole = env.at[site, :, member]

        @pl.when(ahead)
        def _():
            local(whole, env_sent.at[site, 0]).wait()

        @pl.when(behind)
        def _():
            local(whole, env_sent.at[site, 1]).wait()

        for step in range(1, group):
            local(whole, env_sent.at[site, 1 + step]).wait()


def finish_kernel(owners, block, bond, raw_ref, stat_ref, outcome_ref, env_ref, prob_ref, log_ref):
    span = pl.ds(pl.multiple_of(lax.axis_index("inb") * block, block), block)
    means = stat_ref[...] / bond + epsilon
    for site in range(2):
        first = site * owners
        total = means[first : first + 1]
        for r in range(1, owners):
            total = total + means[first + r : first + r + 1]
        ids = outcome_ref[site : site + 1, span]
        for p in range(owners):
            turn = lax.rem(p + owners - ids, owners)
            share = means[first : first + 1]
            for r in range(1, owners):
                share = jnp.where(turn == r, means[first + r : first + r + 1], share)
            prob_ref[site, p : p + 1, :] = share / total
    log_ref[...] = 0.5 * jnp.log(means[0:1]) + 0.5 * jnp.log(means[owners : owners + 1])
    factor = jnp.broadcast_to(lax.rsqrt(means[owners : owners + 1]), (LANES, LANES)).T
    for g in range(raw_ref.shape[1] // LANES):
        cols = slice(g * LANES, (g + 1) * LANES)
        env_ref[:, cols] = raw_ref[:, cols] * factor


def on_device(owners, outs, site_cores, left_env, outcomes):
    samples, width = left_env.shape
    sites, count, depth = site_cores.shape[:3]
    group = outs // owners
    block = samples // owners
    wide = max(LANES, width // 4)
    tiles = width // wide
    chunks = max(owners, PIECES // tiles)
    rows = samples // chunks
    bond = width * outs
    lag = 5
    assert chunks * tiles >= tiles + lag + HOP * (owners - 1) and sites == 2 and count == owners == 4 and block == LANES and depth == group * width
    f32, bf16 = jnp.float32, jnp.bfloat16
    dma = pltpu.SemaphoreType.DMA
    dims = (owners, outs, group, rows, chunks, tiles, wide, bond, lag)
    env_raw, stats = pl.pallas_call(
        functools.partial(sites_kernel, dims),
        out_shape=(jax.ShapeDtypeStruct((block, width), f32), jax.ShapeDtypeStruct((2 * owners, LANES), f32)),
        in_specs=[
            pl.BlockSpec(memory_space=pl.ANY), pl.BlockSpec(memory_space=pl.ANY),
            pl.BlockSpec(memory_space=pltpu.VMEM),
        ],
        out_specs=(pl.BlockSpec(memory_space=pltpu.VMEM), pl.BlockSpec(memory_space=pltpu.VMEM)),
        scratch_shapes=[
            pltpu.VMEM((2, chunks, group, tiles, rows, wide), f32),
            pltpu.VMEM((LANES, LANES), jnp.int32),
            pltpu.VMEM((2 * rows, depth), bf16),
            pltpu.VMEM((tiles + 1, count, depth, wide), bf16),
            pltpu.VMEM((tiles + 1, count, depth, wide), bf16),
            pltpu.VMEM((2, depth, wide), f32),
            pltpu.VMEM((lag, 4, rows, wide), f32),
            pltpu.VMEM((RING, 2, rows, wide), f32),
            pltpu.VMEM((RING, rows, wide), f32),
            pltpu.VMEM((2, chunks, rows, LANES), f32),
            pltpu.VMEM((rows, LANES), f32),
            pltpu.VMEM((chunks, 8, LANES), f32),
            pltpu.VMEM((chunks, owners, 8, LANES), f32),
            pltpu.VMEM((owners, 8, LANES), f32),
            pltpu.VMEM((owners, 8, LANES), f32),
            pltpu.VMEM((2 * owners, LANES), f32),
            pltpu.VMEM((outs, 2 * owners, LANES), f32),
            dma((2, chunks, tiles)), dma((2, chunks, group)), dma((4, tiles)), dma((4, group)), dma((2, 1 + group)),
            dma((lag,)), dma((RING,)), dma((lag,)), dma((RING,)),
            dma((owners,)), dma((chunks, owners)), dma((2,)),
            dma((owners,)), dma((owners,)), dma((outs,)), dma((outs,)),
        ],
        compiler_params=pltpu.CompilerParams(
            collective_id=0, has_side_effects=True, vmem_limit_bytes=62 * 1024 * 1024
        ),
        cost_estimate=pl.CostEstimate(
            flops=12 * samples * depth * count * width, bytes_accessed=8 * count * depth * width, transcendentals=0
        ),
        name="sites",
    )(left_env, site_cores, outcomes)

    spec = pl.BlockSpec(memory_space=pltpu.VMEM)
    env_out, probs, logs = pl.pallas_call(
        functools.partial(finish_kernel, owners, block, bond),
        out_shape=(
            jax.ShapeDtypeStruct((block, width), f32), jax.ShapeDtypeStruct((sites, count, block), f32),
            jax.ShapeDtypeStruct((1, block), f32),
        ),
        in_specs=[spec] * 3,
        out_specs=(spec,) * 3,
        name="finish",
    )(env_raw, stats, outcomes)
    return (env_out, probs, logs.reshape(block))


def solution(mesh):
    in_specs = (P(None, None, "inb", "outb"), P(None, "outb"), P())
    out_specs = (P("inb", "outb"), P(None, None, "inb"), P("inb"))
    return jax.shard_map(
        functools.partial(on_device, mesh.shape["inb"], mesh.shape["outb"]),
        mesh=mesh, in_specs=in_specs, out_specs=out_specs, check_vma=False,
    )
```
